128 devices in a mesh: cd: 8 (over x_hi, y), ab: 16 (over z, x_lo, core).
Axes of the slice: x: 4 (x_hi: 2, x_lo: 2; x = x_hi * 2 + x_lo), y: 4, z: 4, core: 2. Of those that a mesh axis runs over, the one named last changes fastest.
Arguments:
- amplitudes: float32 [1024, 16384], P('ab', 'cd'), may hold values from -6 to 6
- singles: float32 [256, 1024], replicated, may hold values from -3 to 3
- pair_list: int32 [1024, 2], P('ab'), may hold values from 0 to 255
- irrep: int32 [1024], replicated, may hold values from 0 to 7
- block_sizes: int32 [16], replicated, may hold values from 1 to 2, 24 in all
- tile_of_slot: int32 [32], replicated, may hold values from 0 to 511
- integrals: bfloat16 [65536, 16384], P('ab', 'cd'), may hold values from -0.125 to 0.125
Outputs:
- residual: float32 [1024, 65536], P('cd', 'ab')
The draws below stay inside these ranges and needn't reach their ends.
Inputs may be any that keep to these rules, and one draw needn't show every extreme that they name: `block_sizes`: the live slots of an index of ab are its leading ones; the entries sum to 24. `tile_of_slot`: tile t holds the ab pairs whose first orbital is 2 t or 2 t + 1.
All inputs are finite; a program needn't handle non-finite values.
Results may differ from the reference program's by a relative error of at most 0.0029.
Values may be sent and summed in bfloat16 or wider, within the bound.
A program may use at most 128 MiB of HBM per device.

```python
import math
import jax
import jax.numpy as jnp
import numpy as np
from jax import lax

NV = 1024
NO = 256
IJ = 1024
C_DEV = 2
CAP = 2
IRREPS = 8
TAB = 2048
CD = 16384
SLOTS = 32
N_CD = 8
N_AB = 16


def place_ends(array, key, low, top_value):
    index_at = [jax.random.randint(jax.random.fold_in(key, axis), (), 0, length) for axis, length in enumerate(array.shape)]
    longest = array.shape.index(max(array.shape))
    beside = index_at[:longest] + [(index_at[longest] + 1) % array.shape[longest]] + index_at[longest + 1:]
    return array.at[tuple(index_at)].set(low).at[tuple(beside)].set(top_value)


def block_scale(stream_key, extent, shards, least, top_value):
    loudness, own = 1.0, jax.random.fold_in(stream_key, 6)
    for axis_at, blocks in shards:
        draws = jnp.exp(jax.random.uniform(jax.random.fold_in(own, axis_at), (blocks,), jnp.float32, least / len(shards), top_value / len(shards)))
        loudness = loudness * jnp.repeat(draws, extent[axis_at] // blocks).reshape([-1 if axis == axis_at else 1 for axis in range(len(extent))])
    return loudness


def length_profile(count, total, limit, lean):
    portions = [(1 << 20) // math.isqrt(rank ** lean) + 1 for rank in range(2, count + 1)]
    spare, holding = total - limit - (count - 1), [1] * (count - 1)
    while spare > 0:
        movable = [i for i in range(count - 1) if holding[i] < limit]
        whole, left = sum([portions[i] for i in movable]), spare
        for i in movable:
            extra = min(limit - holding[i], max(1, left * portions[i] // whole), spare)
            holding[i] = holding[i] + extra
            spare = spare - extra
    return np.array([limit] + holding)


def uneven(rng, number_of, total, reach, skew):
    if number_of == 2:
        one = jax.random.randint(rng, (), max(1, total - reach), min(reach, total - 1) + 1)
        return jnp.stack([one, total - one])
    tallies = jnp.asarray(length_profile(number_of, total, reach, skew), jnp.int32)
    couples = (number_of - 1) // 2
    giver, sink = tallies[1:1 + 2 * couples:2], tallies[2:2 + 2 * couples:2]
    slack = jnp.minimum(giver - 1, reach - sink)
    shifted = jax.random.randint(jax.random.fold_in(rng, 1), (couples,), 0, 1 << 20) % (slack + 1)
    tallies = tallies.at[1:1 + 2 * couples:2].set(giver - shifted).at[2:2 + 2 * couples:2].set(sink + shifted)
    return tallies[jax.random.permutation(jax.random.fold_in(rng, 2), number_of)]


def scatter_about(own_key, extent, spread, most, cuts=(), kind=jnp.bfloat16):
    drawn = spread * jax.random.normal(own_key, extent, jnp.float32)
    if cuts:
        drawn = drawn * block_scale(own_key, extent, cuts, -0.22, 0.18)
    return jnp.clip(drawn, -most, most).astype(kind)


def setup_inputs(seed: int = 0) -> dict:
    splits = jax.random.split(jax.random.key(seed), 8)
    return {
        "amplitudes": scatter_about(splits[0], (IJ, CD), 1.0, 6.0, ((0, 16), (1, 8)), jnp.float32),
        "singles": scatter_about(splits[1], (NO, NV), 0.5, 3.0, (), jnp.float32),
        "pair_list": place_ends(jax.random.randint(splits[2], (IJ, 2), 0, NO), jax.random.fold_in(splits[2], 1), 0, NO - 1).astype(jnp.int32),
        "irrep": place_ends(jax.random.randint(splits[3], (NV,), 0, IRREPS), jax.random.fold_in(splits[3], 1), 0, IRREPS - 1).astype(jnp.int32),
        "block_sizes": uneven(splits[4], N_AB, N_AB + N_AB // 2, CAP, 2).astype(jnp.int32),
        "tile_of_slot": place_ends(jax.random.randint(splits[5], (SLOTS,), 0, NV // 2), jax.random.fold_in(splits[5], 1), 0, (NV // 2) - 1).astype(jnp.int32),
        "integrals": scatter_about(splits[6], (SLOTS * TAB, CD), (C_DEV * NV * N_CD // 8) ** -0.5, 0.125, ((0, 16), (1, 8))),
    }


def tile_symmetry(tiles, rows, irrep):
    orbitals = irrep.shape[0]
    table = jnp.arange(orbitals, dtype=jnp.int32)
    first = jnp.sum(jnp.where(table[None, :] == 2 * tiles[:, None], irrep[None, :], 0), axis=1)
    second = jnp.sum(jnp.where(table[None, :] == 2 * tiles[:, None] + 1, irrep[None, :], 0), axis=1)
    upper = (rows // orbitals)[None, :]
    leading = jnp.where(upper == 0, first[:, None], second[:, None])
    trailing = jnp.take(irrep, rows % orbitals)
    return jnp.bitwise_xor(leading, trailing[None, :])


def reference(amplitudes, singles, pair_list, irrep, block_sizes, tile_of_slot, integrals):
    orbitals = irrep.shape[0]
    slab = amplitudes.shape[1] // orbitals
    pairs = amplitudes.shape[0]
    left = jnp.take(singles, pair_list[:, 0], axis=0)[:, :slab]
    right = jnp.take(singles, pair_list[:, 1], axis=0)
    combined = amplitudes + (left[:, :, None] * right[:, None, :]).reshape(pairs, slab * orbitals)
    combined_low = combined.astype(jnp.bfloat16)
    column_irrep = jnp.bitwise_xor(irrep[:slab, None], irrep[None, :]).reshape(slab * orbitals)
    tile_rows = 2 * orbitals
    slots = tile_of_slot.shape[0]
    per_owner = slots // N_AB
    blocks = integrals.reshape(slots, tile_rows, slab * orbitals)
    rows = jnp.arange(tile_rows, dtype=jnp.int32)

    def one_slot(index):
        count = block_sizes[index // per_owner]

        def compute(unused):
            symmetry = tile_symmetry(tile_of_slot[index][None], rows, irrep)[0]
            masked = jnp.where(symmetry[:, None] == column_irrep[None, :], blocks[index], jnp.zeros((), jnp.bfloat16))
            return jnp.dot(combined_low, masked.T, preferred_element_type=jnp.float32)

        def empty(unused):
            return jnp.zeros((pairs, tile_rows), jnp.float32)

        return lax.cond(index % per_owner < count, compute, empty, 0)

    parts = lax.map(one_slot, jnp.arange(slots, dtype=jnp.int32))
    return jnp.transpose(parts, (1, 0, 2)).reshape(pairs, slots * tile_rows)
```

```python
import functools

import jax
import jax.numpy as jnp
from jax import lax
from jax.experimental import pallas as pl
from jax.experimental.pallas import tpu as pltpu
from jax.sharding import PartitionSpec as P

MESH = pl.DeviceIdType.MESH
KINDS = 7


def tile_symmetry(tiles, rows, irrep):
    orbitals = irrep.shape[0]
    table = jnp.arange(orbitals, dtype=jnp.int32)
    first = jnp.sum(jnp.where(table[None, :] == 2 * tiles[:, None], irrep[None, :], 0), axis=1)
    second = jnp.sum(jnp.where(table[None, :] == 2 * tiles[:, None] + 1, irrep[None, :], 0), axis=1)
    upper = (rows // orbitals)[None, :]
    leading = jnp.where(upper == 0, first[:, None], second[:, None])
    trailing = jnp.take(irrep, rows % orbitals)
    return jnp.bitwise_xor(leading, trailing[None, :])


def ladder_kernel(
    ring, width, inner,
    tau_any, tiles_any, row_ref, column_ref, out_ref,
    tau, tiles, acc, keep, sent, held,
    tau_sem, tile_sem, send_sem, recv_sem,
):
    chunks = tiles.shape[0]
    rows = out_ref.shape[0]
    me = lax.axis_index("cd")
    y, x = lax.rem(me, ring), lax.div(me, ring)
    up_y, down_y, far_y = lax.rem(y + 1, ring), lax.rem(y + ring - 1, ring), lax.rem(y + 2, ring)
    up, down, across = x * ring + up_y, x * ring + down_y, (1 - x) * ring + y
    targets = (up, down, up, down, up, down, across)

    tau_copy = pltpu.make_async_copy(tau_any, tau, tau_sem)
    tau_copy.start()

    def tile_copy(c):
        return pltpu.make_async_copy(
            tiles_any.at[pl.ds(pl.multiple_of(c * width, width), width), :], tiles.at[c], tile_sem.at[c]
        )

    def remote(kind, c):
        return pltpu.make_async_remote_copy(
            src_ref=sent.at[kind, c],
            dst_ref=held.at[kind, c],
            send_sem=send_sem.at[kind, c],
            recv_sem=recv_sem.at[kind, c],
            device_id={"cd": targets[kind]},
            device_id_type=MESH,
        )

    @pl.loop(0, chunks)
    def _(c):
        tile_copy(c).start()

    barrier = pltpu.get_barrier_semaphore()
    for other in (up, down, across):
        pl.semaphore_signal(barrier, inc=1, device_id={"cd": other}, device_id_type=MESH)
    pl.semaphore_wait(barrier, 3)
    tau_copy.wait()

    def piece(part, block):
        return acc[pl.ds(pl.multiple_of((part * ring + block) * rows, rows), rows), :]

    def multiply(c):
        tile_copy(c).wait()

        @pl.loop(0, width // inner)
        def _(t):
            at = pl.multiple_of(t * inner, inner)
            row = row_ref[pl.ds(pl.multiple_of(c * width + t * inner, inner), inner), :]
            tile = tiles[c, pl.ds(at, inner), :]
            masked = jnp.where(row == column_ref[...], tile, jnp.zeros_like(tile))
            acc[:, pl.ds(at, inner)] = lax.dot_general(
                tau[...], masked, (((1,), (1,)), ((), ())), preferred_element_type=jnp.float32
            )

        for kind, part, block in ((0, 0, far_y), (1, 1, far_y), (2, 1, up_y), (3, 0, down_y)):
            sent[kind, c] = piece(part, block).astype(jnp.bfloat16)
            remote(kind, c).start()
        for slot, part, block in ((0, 0, up_y), (1, 1, down_y), (2, 0, y), (3, 1, y)):
            keep[slot, c] = piece(part, block)

    def relay(c):
        for kind in (0, 1):
            remote(kind, c).wait_recv()
            total = keep[kind, c] + held[kind, c].astype(jnp.float32)
            sent[4 + kind, c] = total.astype(jnp.bfloat16)
            remote(4 + kind, c).start()

    def cross(c):
        for kind in (2, 3, 4, 5):
            remote(kind, c).wait_recv()
        first = keep[2, c] + held[3, c].astype(jnp.float32) + held[4, c].astype(jnp.float32)
        second = keep[3, c] + held[2, c].astype(jnp.float32) + held[5, c].astype(jnp.float32)
        sent[6, c] = jnp.where(x == 0, second, first).astype(jnp.bfloat16)
        remote(6, c).start()
        keep[2, c] = jnp.where(x == 0, first, second)

    def finish(c):
        remote(6, c).wait_recv()
        at = pl.multiple_of(c * width, width)
        out_ref[:, pl.ds(at, width)] = keep[2, c] + held[6, c].astype(jnp.float32)

    @pl.loop(0, chunks + 3)
    def _(i):
        for lag, stage in enumerate((multiply, relay, cross, finish)):
            @pl.when((i >= lag) & (i < chunks + lag))
            def _():
                stage(i - lag)

    @pl.loop(0, chunks)
    def _(c):
        for kind in range(KINDS):
            remote(kind, c).wait_send()


def ladder(ring, tau, integrals, row_symmetry, column_symmetry, width, inner):
    pairs, columns = tau.shape
    rows = pairs // (2 * ring)
    total = integrals.shape[0]
    chunks = total // width
    anywhere = pl.BlockSpec(memory_space=pl.ANY)
    local = pl.BlockSpec(memory_space=pltpu.VMEM)
    return pl.pallas_call(
        functools.partial(ladder_kernel, ring, width, inner),
        out_shape=jax.ShapeDtypeStruct((rows, total), jnp.float32),
        in_specs=[anywhere, anywhere, local, local],
        out_specs=local,
        scratch_shapes=[
            pltpu.VMEM((pairs, columns), jnp.bfloat16),
            pltpu.VMEM((chunks, width, columns), jnp.bfloat16),
            pltpu.VMEM((pairs, width), jnp.float32),
            pltpu.VMEM((4, chunks, rows, width), jnp.float32),
            pltpu.VMEM((KINDS, chunks, rows, width), jnp.bfloat16),
            pltpu.VMEM((KINDS, chunks, rows, width), jnp.bfloat16),
            pltpu.SemaphoreType.DMA,
            pltpu.SemaphoreType.DMA((chunks,)),
            pltpu.SemaphoreType.DMA((KINDS, chunks)),
            pltpu.SemaphoreType.DMA((KINDS, chunks)),
        ],
        compiler_params=pltpu.CompilerParams(
            collective_id=0, has_side_effects=True, vmem_limit_bytes=60 * 1024 * 1024
        ),
    )(tau, integrals, row_symmetry, column_symmetry)


def on_device(amplitudes, singles, pair_list, irrep, block_sizes, tile_of_slot, integrals):
    groups = lax.axis_size("ab")
    ring = lax.axis_size("cd") // 2
    owner_index = lax.axis_index("ab")
    slab_index = lax.axis_index("cd")
    orbitals = irrep.shape[0]
    columns = amplitudes.shape[1]
    slab = columns // orbitals
    local_pairs = amplitudes.shape[0]
    left = jnp.take(singles, pair_list[:, 0], axis=0)
    left = lax.dynamic_slice_in_dim(left, slab_index * slab, slab, 1)
    right = jnp.take(singles, pair_list[:, 1], axis=0)
    combined = amplitudes + (left[:, :, None] * right[:, None, :]).reshape(local_pairs, columns)
    combined_low = combined.astype(jnp.bfloat16)
    piece = lax.all_gather(combined_low, "ab", axis=0, tiled=True)
    slab_irrep = lax.dynamic_slice_in_dim(irrep, slab_index * slab, slab, 0)
    column_irrep = jnp.bitwise_xor(slab_irrep[:, None], irrep[None, :]).reshape(1, columns)
    capacity = tile_of_slot.shape[0] // groups
    tile_rows = integrals.shape[0] // capacity
    count = jnp.take(block_sizes, owner_index)
    tiles = lax.dynamic_slice_in_dim(tile_of_slot, owner_index * capacity, capacity, 0)
    symmetry = tile_symmetry(tiles, jnp.arange(tile_rows, dtype=jnp.int32), irrep)
    live = jnp.arange(capacity, dtype=jnp.int32)[:, None] < count
    symmetry = jnp.where(live, symmetry, -1).reshape(capacity * tile_rows, 1)
    width = min(512, tile_rows // 2)
    return ladder(
        ring, piece, integrals,
        symmetry.astype(jnp.bfloat16), column_irrep.astype(jnp.bfloat16),
        width, min(256, width),
    )


def solution(mesh):
    placed = (P("ab", "cd"), P(), P("ab", None), P(), P(), P(), P("ab", "cd"))
    return jax.shard_map(
        on_device, mesh=mesh, in_specs=placed, out_specs=P("cd", "ab"), check_vma=False
    )
```

```python
import functools

import jax
import jax.numpy as jnp
from jax import lax
from jax.experimental import pallas as pl
from jax.experimental.pallas import tpu as pltpu
from jax.sharding import PartitionSpec as P

MESH = pl.DeviceIdType.MESH
KINDS = 7
HOPS = (
    ((0, 0, 0), 0, (0, 1, 0)),
    ((0, 0, 0), 1, (3, 0, 0)),
    ((0, 0, 0), 2, (1, 0, 0)),
    ((0, 0, 0), 3, (0, 0, 1)),
    ((0, 1, 0), 1, (3, 1, 0)),
    ((0, 1, 0), 2, (1, 1, 0)),
    ((0, 1, 0), 3, (0, 1, 1)),
    ((3, 0, 0), 1, (2, 0, 0)),
    ((3, 0, 0), 3, (3, 0, 1)),
    ((1, 0, 0), 3, (1, 0, 1)),
    ((3, 1, 0), 3, (3, 1, 1)),
    ((1, 1, 0), 2, (2, 1, 0)),
    ((1, 1, 0), 3, (1, 1, 1)),
    ((2, 0, 0), 3, (2, 0, 1)),
    ((2, 1, 0), 3, (2, 1, 1)),
)
RELAYS = ((0, (4, 5, 6)), (1, (7, 8)), (2, (9,)), (4, (10,)), (5, (11, 12)), (7, (13,)), (11, (14,)))


def tile_symmetry(tiles, rows, irrep):
    orbitals = irrep.shape[0]
    table = jnp.arange(orbitals, dtype=jnp.int32)
    first = jnp.sum(jnp.where(table[None, :] == 2 * tiles[:, None], irrep[None, :], 0), axis=1)
    second = jnp.sum(jnp.where(table[None, :] == 2 * tiles[:, None] + 1, irrep[None, :], 0), axis=1)
    upper = (rows // orbitals)[None, :]
    leading = jnp.where(upper == 0, first[:, None], second[:, None])
    trailing = jnp.tile(irrep, rows.shape[0] // orbitals)
    return jnp.bitwise_xor(leading, trailing[None, :])


def ladder_kernel(
    ring, width, inner, parts,
    own_ref, tiles_any, row_ref, column_ref, out_ref,
    tau, tiles, acc, keep, sent, held,
    tile_sem, send_sem, recv_sem, spread_sem, gather_sem,
):
    chunks = tiles.shape[0]
    rows = out_ref.shape[0]
    me = lax.axis_index("cd")
    y, x = lax.rem(me, ring), lax.div(me, ring)
    up_y, down_y, far_y = lax.rem(y + 1, ring), lax.rem(y + ring - 1, ring), lax.rem(y + 2, ring)
    up, down, across = x * ring + up_y, x * ring + down_y, (1 - x) * ring + y
    targets = (up, down, up, down, up, down, across)

    owner = lax.axis_index("ab")
    z, side, core = lax.div(owner, 4), lax.rem(lax.div(owner, 2), 2), lax.rem(owner, 2)
    depth = tau.shape[0] // 16 // parts

    def shard(dz, dx, dk):
        return lax.rem(z + dz, 4) * 4 + lax.rem(side + dx, 2) * 2 + lax.rem(core + dk, 2)

    beside, above, below, twin = shard(0, 1, 0), shard(1, 0, 0), shard(3, 0, 0), shard(0, 0, 1)

    def block(index, part):
        return pl.ds(pl.multiple_of((index * parts + part) * depth, depth), depth)

    def give(hop, part):
        offset, other, _ = HOPS[hop]
        target = (beside, above, below, twin)[other]
        rows_at = block(shard(*offset), part)
        source = tau.at[rows_at, :]
        if offset == (0, 0, 0):
            source = own_ref.at[pl.ds(part * depth, depth), :]
        return pltpu.make_async_remote_copy(
            src_ref=source,
            dst_ref=tau.at[rows_at, :],
            send_sem=spread_sem.at[hop, part],
            recv_sem=gather_sem.at[hop, part],
            device_id={"ab": target},
            device_id_type=MESH,
        )

    def take(hop, part):
        landed = tau.at[block(shard(*HOPS[hop][2]), part), :]
        pltpu.make_async_remote_copy(
            src_ref=landed, dst_ref=landed,
            send_sem=spread_sem.at[hop, part], recv_sem=gather_sem.at[hop, part],
            device_id={"ab": beside}, device_id_type=MESH,
        ).wait_recv()

    def tile_copy(c):
        return pltpu.make_async_copy(
            tiles_any.at[pl.ds(pl.multiple_of(c * width, width), width), :], tiles.at[c], tile_sem.at[c]
        )

    def remote(kind, c):
        return pltpu.make_async_remote_copy(
            src_ref=sent.at[kind, c],
            dst_ref=held.at[kind, c],
            send_sem=send_sem.at[kind, c],
            recv_sem=recv_sem.at[kind, c],
            device_id={"cd": targets[kind]},
            device_id_type=MESH,
        )

    @pl.loop(0, chunks)
    def _(c):
        tile_copy(c).start()

    barrier = pltpu.get_barrier_semaphore()
    for other in (up, down, across):
        pl.semaphore_signal(barrier, inc=1, device_id={"cd": other}, device_id_type=MESH)
    for other in (beside, above, below, twin):
        pl.semaphore_signal(barrier, inc=1, device_id={"ab": other}, device_id_type=MESH)
    pl.semaphore_wait(barrier, 7)

    for hop in (1, 2, 0, 3):
        for part in range(parts):
            give(hop, part).start()
    for part in range(parts):
        tau[block(owner, part), :] = own_ref[part * depth:(part + 1) * depth, :]
    for arrived, onward in RELAYS:
        for part in range(parts):
            take(arrived, part)
            for hop in onward:
                give(hop, part).start()
    for hop in (3, 6, 8, 9, 10, 12, 13, 14):
        for part in range(parts):
            take(hop, part)

    def piece(part, block):
        return acc[pl.ds(pl.multiple_of((part * ring + block) * rows, rows), rows), :]

    def multiply(c):
        tile_copy(c).wait()

        @pl.loop(0, width // inner)
        def _(t):
            at = pl.multiple_of(t * inner, inner)
            row = row_ref[pl.ds(pl.multiple_of(c * width + t * inner, inner), inner), :]
            tile = tiles[c, pl.ds(at, inner), :]
            masked = jnp.where(row == column_ref[...], tile, jnp.zeros_like(tile))
            acc[:, pl.ds(at, inner)] = lax.dot_general(
                tau[...], masked, (((1,), (1,)), ((), ())), preferred_element_type=jnp.float32
            )

        for kind, part, block in ((0, 0, far_y), (1, 1, far_y), (2, 1, up_y), (3, 0, down_y)):
            sent[kind, c] = piece(part, block).astype(jnp.bfloat16)
            remote(kind, c).start()
        for slot, part, block in ((0, 0, up_y), (1, 1, down_y), (2, 0, y), (3, 1, y)):
            keep[slot, c] = piece(part, block)

    def relay(c):
        for kind in (0, 1):
            remote(kind, c).wait_recv()
            total = keep[kind, c] + held[kind, c].astype(jnp.float32)
            sent[4 + kind, c] = total.astype(jnp.bfloat16)
            remote(4 + kind, c).start()

    def cross(c):
        for kind in (2, 3, 4, 5):
            remote(kind, c).wait_recv()
        first = keep[2, c] + held[3, c].astype(jnp.float32) + held[4, c].astype(jnp.float32)
        second = keep[3, c] + held[2, c].astype(jnp.float32) + held[5, c].astype(jnp.float32)
        sent[6, c] = jnp.where(x == 0, second, first).astype(jnp.bfloat16)
        remote(6, c).start()
        keep[2, c] = jnp.where(x == 0, first, second)

    def finish(c):
        remote(6, c).wait_recv()
        at = pl.multiple_of(c * width, width)
        out_ref[:, pl.ds(at, width)] = keep[2, c] + held[6, c].astype(jnp.float32)

    @pl.loop(0, chunks + 3)
    def _(i):
        for lag, stage in enumerate((multiply, relay, cross, finish)):
            @pl.when((i >= lag) & (i < chunks + lag))
            def _():
                stage(i - lag)

    @pl.loop(0, chunks)
    def _(c):
        for kind in range(KINDS):
            remote(kind, c).wait_send()

    for hop in range(len(HOPS)):
        for part in range(parts):
            give(hop, part).wait_send()


def ladder(ring, own, integrals, row_symmetry, column_symmetry, width, inner, parts):
    pairs, columns = own.shape[0] * 16, own.shape[1]
    rows = pairs // (2 * ring)
    total = integrals.shape[0]
    chunks = total // width
    anywhere = pl.BlockSpec(memory_space=pl.ANY)
    local = pl.BlockSpec(memory_space=pltpu.VMEM)
    return pl.pallas_call(
        functools.partial(ladder_kernel, ring, width, inner, parts),
        out_shape=jax.ShapeDtypeStruct((rows, total), jnp.float32),
        in_specs=[local, anywhere, local, local],
        out_specs=local,
        scratch_shapes=[
            pltpu.VMEM((pairs, columns), jnp.bfloat16),
            pltpu.VMEM((chunks, width, columns), jnp.bfloat16),
            pltpu.VMEM((pairs, width), jnp.float32),
            pltpu.VMEM((4, chunks, rows, width), jnp.float32),
            pltpu.VMEM((KINDS, chunks, rows, width), jnp.bfloat16),
            pltpu.VMEM((KINDS, chunks, rows, width), jnp.bfloat16),
            pltpu.SemaphoreType.DMA((chunks,)),
            pltpu.SemaphoreType.DMA((KINDS, chunks)),
            pltpu.SemaphoreType.DMA((KINDS, chunks)),
            pltpu.SemaphoreType.DMA((len(HOPS), parts)),
            pltpu.SemaphoreType.DMA((len(HOPS), parts)),
        ],
        compiler_params=pltpu.CompilerParams(
            collective_id=0, has_side_effects=True, vmem_limit_bytes=60 * 1024 * 1024
        ),
    )(own, integrals, row_symmetry, column_symmetry)


def on_device(amplitudes, singles, pair_list, irrep, block_sizes, tile_of_slot, integrals):
    groups = lax.axis_size("ab")
    ring = lax.axis_size("cd") // 2
    owner_index = lax.axis_index("ab")
    slab_index = lax.axis_index("cd")
    orbitals = irrep.shape[0]
    columns = amplitudes.shape[1]
    slab = columns // orbitals
    local_pairs = amplitudes.shape[0]
    left = jnp.take(singles, pair_list[:, 0], axis=0)
    left = lax.dynamic_slice_in_dim(left, slab_index * slab, slab, 1)
    right = jnp.take(singles, pair_list[:, 1], axis=0)
    combined = amplitudes + (left[:, :, None] * right[:, None, :]).reshape(local_pairs, columns)
    combined_low = combined.astype(jnp.bfloat16)
    slab_irrep = lax.dynamic_slice_in_dim(irrep, slab_index * slab, slab, 0)
    column_irrep = jnp.bitwise_xor(slab_irrep[:, None], irrep[None, :]).reshape(1, columns)
    capacity = tile_of_slot.shape[0] // groups
    tile_rows = integrals.shape[0] // capacity
    count = jnp.take(block_sizes, owner_index)
    tiles = lax.dynamic_slice_in_dim(tile_of_slot, owner_index * capacity, capacity, 0)
    symmetry = tile_symmetry(tiles, jnp.arange(tile_rows, dtype=jnp.int32), irrep)
    live = jnp.arange(capacity, dtype=jnp.int32)[:, None] < count
    symmetry = jnp.where(live, symmetry, -1).reshape(capacity * tile_rows, 1)
    width = min(256, tile_rows // 2)
    return ladder(
        ring, combined_low, integrals,
        symmetry.astype(jnp.bfloat16), column_irrep.astype(jnp.bfloat16),
        width, min(256, width), 2,
    )


def solution(mesh):
    placed = (P("ab", "cd"), P(), P("ab", None), P(), P(), P(), P("ab", "cd"))
    return jax.shard_map(
        on_device, mesh=mesh, in_specs=placed, out_specs=P("cd", "ab"), check_vma=False
    )
```

```python
import functools

import jax
import jax.numpy as jnp
from jax import lax
from jax.experimental import pallas as pl
from jax.experimental.pallas import tpu as pltpu
from jax.sharding import PartitionSpec as P

MESH = pl.DeviceIdType.MESH
KINDS = 7
HOPS = (
    ((0, 0, 0), 0, (0, 1, 0)),
    ((0, 0, 0), 1, (3, 0, 0)),
    ((0, 0, 0), 2, (1, 0, 0)),
    ((0, 0, 0), 3, (0, 0, 1)),
    ((0, 1, 0), 1, (3, 1, 0)),
    ((0, 1, 0), 2, (1, 1, 0)),
    ((0, 1, 0), 3, (0, 1, 1)),
    ((3, 0, 0), 1, (2, 0, 0)),
    ((3, 0, 0), 3, (3, 0, 1)),
    ((1, 0, 0), 3, (1, 0, 1)),
    ((3, 1, 0), 3, (3, 1, 1)),
    ((1, 1, 0), 2, (2, 1, 0)),
    ((1, 1, 0), 3, (1, 1, 1)),
    ((2, 0, 0), 3, (2, 0, 1)),
    ((2, 1, 0), 3, (2, 1, 1)),
)
RELAYS = ((0, (4, 5, 6)), (1, (7, 8)), (2, (9,)), (4, (10,)), (5, (11, 12)), (7, (13,)), (11, (14,)))


def ladder_kernel(
    ring, width, inner, parts,
    amplitudes_ref, singles_ref, table_ref, pairs_ref, irrep_ref, sizes_ref, slots_ref, tiles_any, out_ref,
    tau, tiles, acc, keep, sent, held, own_ref, right, left, trailing, column,
    tile_sem, send_sem, recv_sem, spread_sem, gather_sem,
):
    chunks = tiles.shape[0]
    rows = out_ref.shape[0]
    me = lax.axis_index("cd")
    y, x = lax.rem(me, ring), lax.div(me, ring)
    up_y, down_y, far_y = lax.rem(y + 1, ring), lax.rem(y + ring - 1, ring), lax.rem(y + 2, ring)
    up, down, across = x * ring + up_y, x * ring + down_y, (1 - x) * ring + y
    targets = (up, down, up, down, up, down, across)

    owner = lax.axis_index("ab")
    z, side, core = lax.div(owner, 4), lax.rem(lax.div(owner, 2), 2), lax.rem(owner, 2)
    depth = tau.shape[0] // 16 // parts

    def shard(dz, dx, dk):
        return lax.rem(z + dz, 4) * 4 + lax.rem(side + dx, 2) * 2 + lax.rem(core + dk, 2)

    beside, above, below, twin = shard(0, 1, 0), shard(1, 0, 0), shard(3, 0, 0), shard(0, 0, 1)

    def block(index, part):
        return pl.ds(pl.multiple_of((index * parts + part) * depth, depth), depth)

    def give(hop, part):
        offset, other, _ = HOPS[hop]
        target = (beside, above, below, twin)[other]
        rows_at = block(shard(*offset), part)
        source = tau.at[rows_at, :]
        if offset == (0, 0, 0):
            source = own_ref.at[pl.ds(part * depth, depth), :]
        return pltpu.make_async_remote_copy(
            src_ref=source,
            dst_ref=tau.at[rows_at, :],
            send_sem=spread_sem.at[hop, part],
            recv_sem=gather_sem.at[hop, part],
            device_id={"ab": target},
            device_id_type=MESH,
        )

    def take(hop, part):
        landed = tau.at[block(shard(*HOPS[hop][2]), part), :]
        pltpu.make_async_remote_copy(
            src_ref=landed, dst_ref=landed,
            send_sem=spread_sem.at[hop, part], recv_sem=gather_sem.at[hop, part],
            device_id={"ab": beside}, device_id_type=MESH,
        ).wait_recv()

    def tile_copy(c):
        return pltpu.make_async_copy(
            tiles_any.at[pl.ds(pl.multiple_of(c * width, width), width), :], tiles.at[c], tile_sem.at[c]
        )

    def remote(kind, c):
        return pltpu.make_async_remote_copy(
            src_ref=sent.at[kind, c],
            dst_ref=held.at[kind, c],
            send_sem=send_sem.at[kind, c],
            recv_sem=recv_sem.at[kind, c],
            device_id={"cd": targets[kind]},
            device_id_type=MESH,
        )

    @pl.loop(0, chunks)
    def _(c):
        tile_copy(c).start()

    barrier = pltpu.get_barrier_semaphore()
    for other in (up, down, across):
        pl.semaphore_signal(barrier, inc=1, device_id={"cd": other}, device_id_type=MESH)
    for other in (beside, above, below, twin):
        pl.semaphore_signal(barrier, inc=1, device_id={"ab": other}, device_id_type=MESH)

    orbitals = singles_ref.shape[1]
    slab = tau.shape[1] // orbitals
    capacity = tiles.shape[0] * width // (2 * orbitals)

    occupied = lax.broadcasted_iota(jnp.int32, (own_ref.shape[0], singles_ref.shape[0]), 1)
    for ref, at in ((left, 0), (right, 1)):
        chosen = (occupied == pairs_ref[:, at:at + 1]).astype(jnp.float32)
        ref[...] = jnp.dot(
            chosen, singles_ref[:, :ref.shape[1]],
            precision=lax.Precision.HIGHEST, preferred_element_type=jnp.float32,
        )
    lane = lax.broadcasted_iota(jnp.int32, left.shape, 1)
    for k in range(slab):
        factor = jnp.sum(jnp.where(lane == me * slab + k, left[...], 0.0), axis=1, keepdims=True)
        span = slice(k * orbitals, (k + 1) * orbitals)
        own_ref[:, span] = (amplitudes_ref[:, span] + factor * right[...]).astype(jnp.bfloat16)
    for part in range(parts):
        tau[block(owner, part), :] = own_ref[part * depth:(part + 1) * depth, :]
    pl.semaphore_wait(barrier, 7)

    for hop in (1, 2, 0, 3):
        for part in range(parts):
            give(hop, part).start()

    for row in range(orbitals // 128):
        labels = table_ref[row:row + 1, :]
        spread = jnp.broadcast_to(labels.astype(jnp.float32), (128, 128))
        trailing[row * 128:(row + 1) * 128, :] = spread.T
        for k in range(slab):
            mixed = jnp.bitwise_xor(labels, irrep_ref[me * slab + k])
            column[:, k * orbitals + row * 128:k * orbitals + (row + 1) * 128] = mixed.astype(jnp.float32)
    for arrived, onward in RELAYS:
        for part in range(parts):
            take(arrived, part)
            for hop in onward:
                give(hop, part).start()
    for hop in (3, 6, 8, 9, 10, 12, 13, 14):
        for part in range(parts):
            take(hop, part)

    def piece(part, block):
        return acc[pl.ds(pl.multiple_of((part * ring + block) * rows, rows), rows), :]

    def multiply(c):
        tile_copy(c).wait()

        @pl.loop(0, width // inner)
        def _(t):
            at = pl.multiple_of(t * inner, inner)
            start = c * width + t * inner
            slot = lax.div(start, 2 * orbitals)
            upper = lax.rem(lax.div(start, orbitals), 2)
            leading = irrep_ref[2 * slots_ref[owner * capacity + slot] + upper]
            label = trailing[pl.ds(pl.multiple_of(lax.rem(start, orbitals), inner), inner), 0:1]
            mixed = jnp.bitwise_xor(label.astype(jnp.int32), leading)
            row = jnp.where(slot < sizes_ref[owner], mixed, -1).astype(jnp.float32).astype(jnp.bfloat16)
            tile = tiles[c, pl.ds(at, inner), :]
            masked = jnp.where(row == column[...].astype(jnp.bfloat16), tile, jnp.zeros_like(tile))
            acc[:, pl.ds(at, inner)] = lax.dot_general(
                tau[...], masked, (((1,), (1,)), ((), ())), preferred_element_type=jnp.float32
            )

        for kind, part, block in ((0, 0, far_y), (1, 1, far_y), (2, 1, up_y), (3, 0, down_y)):
            sent[kind, c] = piece(part, block).astype(jnp.bfloat16)
            remote(kind, c).start()
        for slot, part, block in ((0, 0, up_y), (1, 1, down_y), (2, 0, y), (3, 1, y)):
            keep[slot, c] = piece(part, block)

    def relay(c):
        for kind in (0, 1):
            remote(kind, c).wait_recv()
            total = keep[kind, c] + held[kind, c].astype(jnp.float32)
            sent[4 + kind, c] = total.astype(jnp.bfloat16)
            remote(4 + kind, c).start()

    def cross(c):
        for kind in (2, 3, 4, 5):
            remote(kind, c).wait_recv()
        first = keep[2, c] + held[3, c].astype(jnp.float32) + held[4, c].astype(jnp.float32)
        second = keep[3, c] + held[2, c].astype(jnp.float32) + held[5, c].astype(jnp.float32)
        sent[6, c] = jnp.where(x == 0, second, first).astype(jnp.bfloat16)
        remote(6, c).start()
        keep[2, c] = jnp.where(x == 0, first, second)

    def finish(c):
        remote(6, c).wait_recv()
        at = pl.multiple_of(c * width, width)
        out_ref[:, pl.ds(at, width)] = keep[2, c] + held[6, c].astype(jnp.float32)

    @pl.loop(0, chunks + 3)
    def _(i):
        for lag, stage in enumerate((multiply, relay, cross, finish)):
            @pl.when((i >= lag) & (i < chunks + lag))
            def _():
                stage(i - lag)

    @pl.loop(0, chunks)
    def _(c):
        for kind in range(KINDS):
            remote(kind, c).wait_send()

    for hop in range(len(HOPS)):
        for part in range(parts):
            give(hop, part).wait_send()


def on_device(amplitudes, singles, pair_list, irrep, block_sizes, tile_of_slot, integrals):
    groups = lax.axis_size("ab")
    ring = lax.axis_size("cd") // 2
    local_pairs, columns = amplitudes.shape
    orbitals = irrep.shape[0]
    pairs = local_pairs * groups
    rows = pairs // (2 * ring)
    total = integrals.shape[0]
    width = min(256, orbitals)
    parts = 2
    chunks = total // width
    anywhere = pl.BlockSpec(memory_space=pl.ANY)
    local = pl.BlockSpec(memory_space=pltpu.VMEM)
    scalars = pl.BlockSpec(memory_space=pltpu.SMEM)
    return pl.pallas_call(
        functools.partial(ladder_kernel, ring, width, min(256, width), parts),
        out_shape=jax.ShapeDtypeStruct((rows, total), jnp.float32),
        in_specs=[local, local, local, local, scalars, scalars, scalars, anywhere],
        out_specs=local,
        scratch_shapes=[
            pltpu.VMEM((pairs, columns), jnp.bfloat16),
            pltpu.VMEM((chunks, width, columns), jnp.bfloat16),
            pltpu.VMEM((pairs, width), jnp.float32),
            pltpu.VMEM((4, chunks, rows, width), jnp.float32),
            pltpu.VMEM((KINDS, chunks, rows, width), jnp.bfloat16),
            pltpu.VMEM((KINDS, chunks, rows, width), jnp.bfloat16),
            pltpu.VMEM((local_pairs, columns), jnp.bfloat16),
            pltpu.VMEM((local_pairs, orbitals), jnp.float32),
            pltpu.VMEM((local_pairs, 128), jnp.float32),
            pltpu.VMEM((orbitals, 128), jnp.float32),
            pltpu.VMEM((1, columns), jnp.float32),
            pltpu.SemaphoreType.DMA((chunks,)),
            pltpu.SemaphoreType.DMA((KINDS, chunks)),
            pltpu.SemaphoreType.DMA((KINDS, chunks)),
            pltpu.SemaphoreType.DMA((len(HOPS), parts)),
            pltpu.SemaphoreType.DMA((len(HOPS), parts)),
        ],
        compiler_params=pltpu.CompilerParams(
            collective_id=0, has_side_effects=True, vmem_limit_bytes=60 * 1024 * 1024
        ),
    )(
        amplitudes, singles, irrep.reshape(orbitals // 128, 128), pair_list,
        irrep, block_sizes, tile_of_slot, integrals,
    )


def solution(mesh):
    placed = (P("ab", "cd"), P(), P("ab", None), P(), P(), P(), P("ab", "cd"))
    return jax.shard_map(
        on_device, mesh=mesh, in_specs=placed, out_specs=P("cd", "ab"), check_vma=False
    )
```

```python
import functools

import jax
import jax.numpy as jnp
from jax import lax
from jax.experimental import pallas as pl
from jax.experimental.pallas import tpu as pltpu
from jax.sharding import PartitionSpec as P

MESH = pl.DeviceIdType.MESH
KINDS = 7
LAG = 2
HOPS = (
    ((0, 0, 0), 0, (0, 1, 0)),
    ((0, 0, 0), 1, (3, 0, 0)),
    ((0, 0, 0), 2, (1, 0, 0)),
    ((0, 0, 0), 3, (0, 0, 1)),
    ((0, 1, 0), 1, (3, 1, 0)),
    ((0, 1, 0), 2, (1, 1, 0)),
    ((0, 1, 0), 3, (0, 1, 1)),
    ((3, 0, 0), 1, (2, 0, 0)),
    ((3, 0, 0), 3, (3, 0, 1)),
    ((1, 0, 0), 3, (1, 0, 1)),
    ((3, 1, 0), 3, (3, 1, 1)),
    ((1, 1, 0), 2, (2, 1, 0)),
    ((1, 1, 0), 3, (1, 1, 1)),
    ((2, 0, 0), 3, (2, 0, 1)),
    ((2, 1, 0), 3, (2, 1, 1)),
)
RELAYS = ((0, (4, 5, 6)), (1, (7, 8)), (2, (9,)), (4, (10,)), (5, (11, 12)), (7, (13,)), (11, (14,)))


def ladder_kernel(
    ring, width, inner, parts,
    amplitudes_ref, singles_ref, table_ref, pairs_ref, irrep_ref, sizes_ref, slots_ref, tiles_any, out_ref,
    tau, tiles, acc, keep, sent, held, sent_far, held_far, own_ref, right, left, trailing, column,
    tile_sem, send_sem, recv_sem, spread_sem, gather_sem,
):
    chunks = tiles.shape[0]
    rows = out_ref.shape[0]
    me = lax.axis_index("cd")
    y, x = lax.rem(me, ring), lax.div(me, ring)
    up_y, down_y, far_y = lax.rem(y + 1, ring), lax.rem(y + ring - 1, ring), lax.rem(y + 2, ring)
    up, down, across = x * ring + up_y, x * ring + down_y, (1 - x) * ring + y
    targets = (up, down, up, down, up, down, across)

    owner = lax.axis_index("ab")
    z, side, core = lax.div(owner, 4), lax.rem(lax.div(owner, 2), 2), lax.rem(owner, 2)
    depth = tau.shape[0] // 16 // parts

    def shard(dz, dx, dk):
        return lax.rem(z + dz, 4) * 4 + lax.rem(side + dx, 2) * 2 + lax.rem(core + dk, 2)

    beside, above, below, twin = shard(0, 1, 0), shard(1, 0, 0), shard(3, 0, 0), shard(0, 0, 1)

    def block(index, part):
        return pl.ds(pl.multiple_of((index * parts + part) * depth, depth), depth)

    def give(hop, part):
        offset, other, _ = HOPS[hop]
        target = (beside, above, below, twin)[other]
        rows_at = block(shard(*offset), part)
        source = tau.at[rows_at, :]
        if offset == (0, 0, 0):
            source = own_ref.at[pl.ds(part * depth, depth), :]
        return pltpu.make_async_remote_copy(
            src_ref=source,
            dst_ref=tau.at[rows_at, :],
            send_sem=spread_sem.at[hop, part],
            recv_sem=gather_sem.at[hop, part],
            device_id={"ab": target},
            device_id_type=MESH,
        )

    def take(hop, part):
        landed = tau.at[block(shard(*HOPS[hop][2]), part), :]
        pltpu.make_async_remote_copy(
            src_ref=landed, dst_ref=landed,
            send_sem=spread_sem.at[hop, part], recv_sem=gather_sem.at[hop, part],
            device_id={"ab": beside}, device_id_type=MESH,
        ).wait_recv()

    def tile_copy(c):
        return pltpu.make_async_copy(
            tiles_any.at[pl.ds(pl.multiple_of(c * width, width), width), :], tiles.at[c], tile_sem.at[c]
        )

    def remote(kind, c):
        return pltpu.make_async_remote_copy(
            src_ref=sent.at[kind, c],
            dst_ref=held.at[kind, c],
            send_sem=send_sem.at[kind, c],
            recv_sem=recv_sem.at[kind, c],
            device_id={"cd": targets[kind]},
            device_id_type=MESH,
        )

    half = rows // 2

    def remote_half(kind, c):
        return pltpu.make_async_remote_copy(
            src_ref=sent.at[kind, c, pl.ds(0, half), :],
            dst_ref=held.at[kind, c, pl.ds(0, half), :],
            send_sem=send_sem.at[kind, c],
            recv_sem=recv_sem.at[kind, c],
            device_id={"cd": targets[kind]},
            device_id_type=MESH,
        )

    def remote_far(c):
        return pltpu.make_async_remote_copy(
            src_ref=sent_far.at[lax.div(c, 2)],
            dst_ref=held_far.at[lax.div(c, 2)],
            send_sem=send_sem.at[6, c],
            recv_sem=recv_sem.at[6, c],
            device_id={"cd": across},
            device_id_type=MESH,
        )

    def across_first(c):
        return (lax.rem(c, 2) == 1) & (c < chunks - 2)

    @pl.loop(0, chunks)
    def _(c):
        tile_copy(c).start()

    barrier = pltpu.get_barrier_semaphore()
    for other in (up, down, across):
        pl.semaphore_signal(barrier, inc=1, device_id={"cd": other}, device_id_type=MESH)
    for other in (beside, above, below, twin):
        pl.semaphore_signal(barrier, inc=1, device_id={"ab": other}, device_id_type=MESH)

    orbitals = singles_ref.shape[1]
    slab = tau.shape[1] // orbitals
    capacity = tiles.shape[0] * width // (2 * orbitals)

    occupied = lax.broadcasted_iota(jnp.int32, (own_ref.shape[0], singles_ref.shape[0]), 1)
    for ref, at in ((left, 0), (right, 1)):
        chosen = (occupied == pairs_ref[:, at:at + 1]).astype(jnp.float32)
        ref[...] = jnp.dot(
            chosen, singles_ref[:, :ref.shape[1]],
            precision=lax.Precision.HIGHEST, preferred_element_type=jnp.float32,
        )
    lane = lax.broadcasted_iota(jnp.int32, left.shape, 1)
    for k in range(slab):
        factor = jnp.sum(jnp.where(lane == me * slab + k, left[...], 0.0), axis=1, keepdims=True)
        span = slice(k * orbitals, (k + 1) * orbitals)
        own_ref[:, span] = (amplitudes_ref[:, span] + factor * right[...]).astype(jnp.bfloat16)
    for part in range(parts):
        tau[block(owner, part), :] = own_ref[part * depth:(part + 1) * depth, :]
    pl.semaphore_wait(barrier, 7)

    for hop in (1, 2, 0, 3):
        for part in range(parts):
            give(hop, part).start()

    for row in range(orbitals // 128):
        labels = table_ref[row:row + 1, :]
        spread = jnp.broadcast_to(labels.astype(jnp.float32), (128, 128))
        trailing[row * 128:(row + 1) * 128, :] = spread.T
        for k in range(slab):
            mixed = jnp.bitwise_xor(labels, irrep_ref[me * slab + k])
            column[:, k * orbitals + row * 128:k * orbitals + (row + 1) * 128] = mixed.astype(jnp.float32)
    for arrived, onward in RELAYS:
        for part in range(parts):
            take(arrived, part)
            for hop in onward:
                give(hop, part).start()
    for hop in (3, 6, 8, 9, 10, 12, 13, 14):
        for part in range(parts):
            take(hop, part)

    def piece(part, block):
        return acc[pl.ds(pl.multiple_of((part * ring + block) * rows, rows), rows), :]

    def multiply(c):
        tile_copy(c).wait()

        @pl.loop(0, width // inner)
        def _(t):
            at = pl.multiple_of(t * inner, inner)
            start = c * width + t * inner
            slot = lax.div(start, 2 * orbitals)
            upper = lax.rem(lax.div(start, orbitals), 2)
            leading = irrep_ref[2 * slots_ref[owner * capacity + slot] + upper]
            label = trailing[pl.ds(pl.multiple_of(lax.rem(start, orbitals), inner), inner), 0:1]
            mixed = jnp.bitwise_xor(label.astype(jnp.int32), leading)
            row = jnp.where(slot < sizes_ref[owner], mixed, -1).astype(jnp.float32).astype(jnp.bfloat16)
            tile = tiles[c, pl.ds(at, inner), :]
            masked = jnp.where(row == column[...].astype(jnp.bfloat16), tile, jnp.zeros_like(tile))
            acc[:, pl.ds(at, inner)] = lax.dot_general(
                tau[...], masked, (((1,), (1,)), ((), ())), preferred_element_type=jnp.float32
            )

        @pl.when(across_first(c))
        def _():
            for step in range(4):
                at_y = lax.rem(y + step, ring)
                sent_far[lax.div(c, 2), step] = piece(1 - x, at_y).astype(jnp.bfloat16)
            remote_far(c).start()
            for step in range(4):
                keep[step, c] = piece(x, lax.rem(y + step, ring))

        @pl.when(jnp.logical_not(across_first(c)))
        def _():
            for kind, part, block in ((0, 0, far_y), (1, 1, far_y), (2, 1, up_y), (3, 0, down_y)):
                sent[kind, c] = piece(part, block).astype(jnp.bfloat16)
                remote(kind, c).start()
            for slot, part, block in ((0, 0, up_y), (1, 1, down_y), (2, 0, y), (3, 1, y)):
                keep[slot, c] = piece(part, block)

    def relay(c):
        for kind in (0, 1):
            remote(kind, c).wait_recv()
            total = keep[kind, c] + held[kind, c].astype(jnp.float32)
            sent[4 + kind, c] = total.astype(jnp.bfloat16)
            remote(4 + kind, c).start()

    def cross(c):
        for kind in (2, 3, 4, 5):
            remote(kind, c).wait_recv()
        first = keep[2, c] + held[3, c].astype(jnp.float32) + held[4, c].astype(jnp.float32)
        second = keep[3, c] + held[2, c].astype(jnp.float32) + held[5, c].astype(jnp.float32)
        sent[6, c] = jnp.where(x == 0, second, first).astype(jnp.bfloat16)
        remote(6, c).start()
        keep[2, c] = jnp.where(x == 0, first, second)

    def finish(c):
        remote(6, c).wait_recv()
        at = pl.multiple_of(c * width, width)
        out_ref[:, pl.ds(at, width)] = keep[2, c] + held[6, c].astype(jnp.float32)

    low, high = slice(0, half), slice(half, rows)

    def fan(c):
        remote_far(c).wait_recv()

        def total(step, span):
            return keep[step, c, span, :] + held_far[lax.div(c, 2), step, span, :].astype(jnp.float32)

        for kind, step, span in ((0, 2, low), (1, 2, high), (2, 1, high), (3, 3, low)):
            sent[kind, c, 0:half, :] = total(step, span).astype(jnp.bfloat16)
            remote_half(kind, c).start()
        for step, span in ((1, low), (3, high), (0, low), (0, high)):
            keep[step, c, span, :] = total(step, span)

    def relay_half(c):
        for kind, step, span in ((0, 1, low), (1, 3, high)):
            remote_half(kind, c).wait_recv()
            total = keep[step, c, span, :] + held[kind, c, 0:half, :].astype(jnp.float32)
            sent[4 + kind, c, 0:half, :] = total.astype(jnp.bfloat16)
            remote_half(4 + kind, c).start()

    def finish_half(c):
        for kind in (2, 3, 4, 5):
            remote_half(kind, c).wait_recv()
        at = pl.multiple_of(c * width, width)
        for direct, relayed, span in ((3, 4, low), (2, 5, high)):
            near = held[direct, c, 0:half, :].astype(jnp.float32)
            out_ref[span, pl.ds(at, width)] = keep[0, c, span, :] + near + held[relayed, c, 0:half, :].astype(jnp.float32)

    @pl.loop(0, chunks + 3 * LAG)
    def _(i):
        @pl.when(i < chunks)
        def _():
            multiply(i)

        for order, pair in enumerate(((relay, fan), (cross, relay_half), (finish, finish_half))):
            lag = LAG * (order + 1)
            c = i - lag
            inside = (i >= lag) & (c < chunks)

            @pl.when(inside & across_first(c))
            def _():
                pair[1](c)

            @pl.when(inside & jnp.logical_not(across_first(c)))
            def _():
                pair[0](c)

    @pl.loop(0, chunks)
    def _(c):
        @pl.when(across_first(c))
        def _():
            remote_far(c).wait_send()
            for kind in range(6):
                remote_half(kind, c).wait_send()

        @pl.when(jnp.logical_not(across_first(c)))
        def _():
            for kind in range(KINDS):
                remote(kind, c).wait_send()

    for hop in range(len(HOPS)):
        for part in range(parts):
            give(hop, part).wait_send()


def on_device(amplitudes, singles, pair_list, irrep, block_sizes, tile_of_slot, integrals):
    groups = lax.axis_size("ab")
    ring = lax.axis_size("cd") // 2
    local_pairs, columns = amplitudes.shape
    orbitals = irrep.shape[0]
    pairs = local_pairs * groups
    rows = pairs // (2 * ring)
    total = integrals.shape[0]
    width = min(256, orbitals)
    parts = 2
    chunks = total // width
    anywhere = pl.BlockSpec(memory_space=pl.ANY)
    local = pl.BlockSpec(memory_space=pltpu.VMEM)
    scalars = pl.BlockSpec(memory_space=pltpu.SMEM)
    return pl.pallas_call(
        functools.partial(ladder_kernel, ring, width, min(256, width), parts),
        out_shape=jax.ShapeDtypeStruct((rows, total), jnp.float32),
        in_specs=[local, local, local, local, scalars, scalars, scalars, anywhere],
        out_specs=local,
        scratch_shapes=[
            pltpu.VMEM((pairs, columns), jnp.bfloat16),
            pltpu.VMEM((chunks, width, columns), jnp.bfloat16),
            pltpu.VMEM((pairs, width), jnp.float32),
            pltpu.VMEM((4, chunks, rows, width), jnp.float32),
            pltpu.VMEM((KINDS, chunks, rows, width), jnp.bfloat16),
            pltpu.VMEM((KINDS, chunks, rows, width), jnp.bfloat16),
            pltpu.VMEM((chunks // 2, ring, rows, width), jnp.bfloat16),
            pltpu.VMEM((chunks // 2, ring, rows, width), jnp.bfloat16),
            pltpu.VMEM((local_pairs, columns), jnp.bfloat16),
            pltpu.VMEM((local_pairs, orbitals), jnp.float32),
            pltpu.VMEM((local_pairs, 128), jnp.float32),
            pltpu.VMEM((orbitals, 128), jnp.float32),
            pltpu.VMEM((1, columns), jnp.float32),
            pltpu.SemaphoreType.DMA((chunks,)),
            pltpu.SemaphoreType.DMA((KINDS, chunks)),
            pltpu.SemaphoreType.DMA((KINDS, chunks)),
            pltpu.SemaphoreType.DMA((len(HOPS), parts)),
            pltpu.SemaphoreType.DMA((len(HOPS), parts)),
        ],
        compiler_params=pltpu.CompilerParams(
            collective_id=0, has_side_effects=True, vmem_limit_bytes=60 * 1024 * 1024
        ),
    )(
        amplitudes, singles, irrep.reshape(orbitals // 128, 128), pair_list,
        irrep, block_sizes, tile_of_slot, integrals,
    )


def solution(mesh):
    placed = (P("ab", "cd"), P(), P("ab", None), P(), P(), P(), P("ab", "cd"))
    return jax.shard_map(
        on_device, mesh=mesh, in_specs=placed, out_specs=P("cd", "ab"), check_vma=False
    )
```

```python
import functools

import jax
import jax.numpy as jnp
from jax import lax
from jax.experimental import pallas as pl
from jax.experimental.pallas import tpu as pltpu
from jax.sharding import PartitionSpec as P

MESH = pl.DeviceIdType.MESH
KINDS = 7
LAG = 8
HOPS = (
    ((0, 0, 0), 0, (0, 1, 0)),
    ((0, 0, 0), 1, (3, 0, 0)),
    ((0, 0, 0), 2, (1, 0, 0)),
    ((0, 0, 0), 3, (0, 0, 1)),
    ((0, 1, 0), 1, (3, 1, 0)),
    ((0, 1, 0), 2, (1, 1, 0)),
    ((0, 1, 0), 3, (0, 1, 1)),
    ((3, 0, 0), 1, (2, 0, 0)),
    ((3, 0, 0), 3, (3, 0, 1)),
    ((1, 0, 0), 3, (1, 0, 1)),
    ((3, 1, 0), 3, (3, 1, 1)),
    ((1, 1, 0), 2, (2, 1, 0)),
    ((1, 1, 0), 3, (1, 1, 1)),
    ((2, 0, 0), 3, (2, 0, 1)),
    ((2, 1, 0), 3, (2, 1, 1)),
)
RELAYS = ((0, (4, 5, 6)), (1, (7, 8)), (2, (9,)), (4, (10,)), (5, (11, 12)), (7, (13,)), (11, (14,)))


def ladder_kernel(
    ring, width, inner, parts,
    amplitudes_ref, singles_ref, table_ref, pairs_ref, irrep_ref, sizes_ref, slots_ref, tiles_any, out_ref,
    tau, tiles, acc, keep, sent, held, sent_far, held_far, own_ref, right, left, trailing, column,
    tile_sem, send_sem, recv_sem, spread_sem, gather_sem,
):
    chunks = tiles.shape[0]
    rows = out_ref.shape[0]
    me = lax.axis_index("cd")
    y, x = lax.rem(me, ring), lax.div(me, ring)
    up_y, down_y, far_y = lax.rem(y + 1, ring), lax.rem(y + ring - 1, ring), lax.rem(y + 2, ring)
    up, down, across = x * ring + up_y, x * ring + down_y, (1 - x) * ring + y
    targets = (up, down, up, down, up, down, across)

    owner = lax.axis_index("ab")
    z, side, core = lax.div(owner, 4), lax.rem(lax.div(owner, 2), 2), lax.rem(owner, 2)
    depth = tau.shape[0] // 16 // parts

    def shard(dz, dx, dk):
        return lax.rem(z + dz, 4) * 4 + lax.rem(side + dx, 2) * 2 + lax.rem(core + dk, 2)

    beside, above, below, twin = shard(0, 1, 0), shard(1, 0, 0), shard(3, 0, 0), shard(0, 0, 1)

    def block(index, part):
        return pl.ds(pl.multiple_of((index * parts + part) * depth, depth), depth)

    def give(hop, part):
        offset, other, _ = HOPS[hop]
        target = (beside, above, below, twin)[other]
        rows_at = block(shard(*offset), part)
        source = tau.at[rows_at, :]
        if offset == (0, 0, 0):
            source = own_ref.at[pl.ds(part * depth, depth), :]
        return pltpu.make_async_remote_copy(
            src_ref=source,
            dst_ref=tau.at[rows_at, :],
            send_sem=spread_sem.at[hop, part],
            recv_sem=gather_sem.at[hop, part],
            device_id={"ab": target},
            device_id_type=MESH,
        )

    def take(hop, part):
        landed = tau.at[block(shard(*HOPS[hop][2]), part), :]
        pltpu.make_async_remote_copy(
            src_ref=landed, dst_ref=landed,
            send_sem=spread_sem.at[hop, part], recv_sem=gather_sem.at[hop, part],
            device_id={"ab": beside}, device_id_type=MESH,
        ).wait_recv()

    def tile_copy(c):
        return pltpu.make_async_copy(
            tiles_any.at[pl.ds(pl.multiple_of(c * width, width), width), :], tiles.at[c], tile_sem.at[c]
        )

    def remote(kind, c):
        return pltpu.make_async_remote_copy(
            src_ref=sent.at[kind, c],
            dst_ref=held.at[kind, c],
            send_sem=send_sem.at[kind, c],
            recv_sem=recv_sem.at[kind, c],
            device_id={"cd": targets[kind]},
            device_id_type=MESH,
        )

    half = rows // 2

    def remote_half(kind, c):
        return pltpu.make_async_remote_copy(
            src_ref=sent.at[kind, c, pl.ds(0, half), :],
            dst_ref=held.at[kind, c, pl.ds(0, half), :],
            send_sem=send_sem.at[kind, c],
            recv_sem=recv_sem.at[kind, c],
            device_id={"cd": targets[kind]},
            device_id_type=MESH,
        )

    def remote_far(c):
        return pltpu.make_async_remote_copy(
            src_ref=sent_far.at[lax.div(c, 2)],
            dst_ref=held_far.at[lax.div(c, 2)],
            send_sem=send_sem.at[6, c],
            recv_sem=recv_sem.at[6, c],
            device_id={"cd": across},
            device_id_type=MESH,
        )

    def across_first(c):
        return (lax.rem(c, 2) == 1) & (c < chunks - 2)

    @pl.loop(0, chunks)
    def _(c):
        tile_copy(c).start()

    barrier = pltpu.get_barrier_semaphore()
    for other in (up, down, across):
        pl.semaphore_signal(barrier, inc=1, device_id={"cd": other}, device_id_type=MESH)
    for other in (beside, above, below, twin):
        pl.semaphore_signal(barrier, inc=1, device_id={"ab": other}, device_id_type=MESH)

    orbitals = singles_ref.shape[1]
    slab = tau.shape[1] // orbitals
    capacity = tiles.shape[0] * width // (2 * orbitals)

    occupied = lax.broadcasted_iota(jnp.int32, (own_ref.shape[0], singles_ref.shape[0]), 1)
    for ref, at in ((left, 0), (right, 1)):
        chosen = (occupied == pairs_ref[:, at:at + 1]).astype(jnp.float32)
        ref[...] = jnp.dot(
            chosen, singles_ref[:, :ref.shape[1]],
            precision=lax.Precision.HIGHEST, preferred_element_type=jnp.float32,
        )
    lane = lax.broadcasted_iota(jnp.int32, left.shape, 1)
    for k in range(slab):
        factor = jnp.sum(jnp.where(lane == me * slab + k, left[...], 0.0), axis=1, keepdims=True)
        span = slice(k * orbitals, (k + 1) * orbitals)
        own_ref[:, span] = (amplitudes_ref[:, span] + factor * right[...]).astype(jnp.bfloat16)
    for part in range(parts):
        tau[block(owner, part), :] = own_ref[part * depth:(part + 1) * depth, :]
    pl.semaphore_wait(barrier, 7)

    for hop in (1, 2, 0, 3):
        for part in range(parts):
            give(hop, part).start()

    for row in range(orbitals // 128):
        labels = table_ref[row:row + 1, :]
        spread = jnp.broadcast_to(labels.astype(jnp.float32), (128, 128))
        trailing[row * 128:(row + 1) * 128, :] = spread.T
        for k in range(slab):
            mixed = jnp.bitwise_xor(labels, irrep_ref[me * slab + k])
            column[:, k * orbitals + row * 128:k * orbitals + (row + 1) * 128] = mixed.astype(jnp.float32)
    for arrived, onward in RELAYS:
        for part in range(parts):
            take(arrived, part)
            for hop in onward:
                give(hop, part).start()
    for hop in (3, 6, 8, 9, 10, 12, 13, 14):
        for part in range(parts):
            take(hop, part)

    def piece(part, block):
        return acc[pl.ds(pl.multiple_of((part * ring + block) * rows, rows), rows), :]

    def multiply(c):
        tile_copy(c).wait()

        @pl.loop(0, width // inner)
        def _(t):
            at = pl.multiple_of(t * inner, inner)
            start = c * width + t * inner
            slot = lax.div(start, 2 * orbitals)
            upper = lax.rem(lax.div(start, orbitals), 2)
            leading = irrep_ref[2 * slots_ref[owner * capacity + slot] + upper]
            label = trailing[pl.ds(pl.multiple_of(lax.rem(start, orbitals), inner), inner), 0:1]
            mixed = jnp.bitwise_xor(label.astype(jnp.int32), leading)
            row = jnp.where(slot < sizes_ref[owner], mixed, -1).astype(jnp.float32).astype(jnp.bfloat16)
            tile = tiles[c, pl.ds(at, inner), :]
            masked = jnp.where(row == column[...].astype(jnp.bfloat16), tile, jnp.zeros_like(tile))
            acc[:, pl.ds(at, inner)] = lax.dot_general(
                tau[...], masked, (((1,), (1,)), ((), ())), preferred_element_type=jnp.float32
            )

        @pl.when(across_first(c))
        def _():
            for step in range(4):
                at_y = lax.rem(y + step, ring)
                sent_far[lax.div(c, 2), step] = piece(1 - x, at_y).astype(jnp.bfloat16)
            remote_far(c).start()
            for step in range(4):
                keep[step, c] = piece(x, lax.rem(y + step, ring))

        @pl.when(jnp.logical_not(across_first(c)))
        def _():
            for kind, part, block in ((0, 0, far_y), (1, 1, far_y), (2, 1, up_y), (3, 0, down_y)):
                sent[kind, c] = piece(part, block).astype(jnp.bfloat16)
                remote(kind, c).start()
            for slot, part, block in ((0, 0, up_y), (1, 1, down_y), (2, 0, y), (3, 1, y)):
                keep[slot, c] = piece(part, block)

    def relay(c):
        for kind in (0, 1):
            remote(kind, c).wait_recv()
            total = keep[kind, c] + held[kind, c].astype(jnp.float32)
            sent[4 + kind, c] = total.astype(jnp.bfloat16)
            remote(4 + kind, c).start()

    def cross(c):
        for kind in (2, 3, 4, 5):
            remote(kind, c).wait_recv()
        first = keep[2, c] + held[3, c].astype(jnp.float32) + held[4, c].astype(jnp.float32)
        second = keep[3, c] + held[2, c].astype(jnp.float32) + held[5, c].astype(jnp.float32)
        sent[6, c] = jnp.where(x == 0, second, first).astype(jnp.bfloat16)
        remote(6, c).start()
        keep[2, c] = jnp.where(x == 0, first, second)

    def finish(c):
        remote(6, c).wait_recv()
        at = pl.multiple_of(c * width, width)
        out_ref[:, pl.ds(at, width)] = keep[2, c] + held[6, c].astype(jnp.float32)

    low, high = slice(0, half), slice(half, rows)

    def fan(c):
        remote_far(c).wait_recv()

        def total(step, span):
            return keep[step, c, span, :] + held_far[lax.div(c, 2), step, span, :].astype(jnp.float32)

        for kind, step, span in ((0, 2, low), (1, 2, high), (2, 1, high), (3, 3, low)):
            sent[kind, c, 0:half, :] = total(step, span).astype(jnp.bfloat16)
            remote_half(kind, c).start()
        for step, span in ((1, low), (3, high), (0, low), (0, high)):
            keep[step, c, span, :] = total(step, span)

    def relay_half(c):
        for kind, step, span in ((0, 1, low), (1, 3, high)):
            remote_half(kind, c).wait_recv()
            total = keep[step, c, span, :] + held[kind, c, 0:half, :].astype(jnp.float32)
            sent[4 + kind, c, 0:half, :] = total.astype(jnp.bfloat16)
            remote_half(4 + kind, c).start()

    def finish_half(c):
        for kind in (2, 3, 4, 5):
            remote_half(kind, c).wait_recv()
        at = pl.multiple_of(c * width, width)
        for direct, relayed, span in ((3, 4, low), (2, 5, high)):
            near = held[direct, c, 0:half, :].astype(jnp.float32)
            out_ref[span, pl.ds(at, width)] = keep[0, c, span, :] + near + held[relayed, c, 0:half, :].astype(jnp.float32)

    @pl.loop(0, chunks + 3 * LAG)
    def _(i):
        @pl.when(i < chunks)
        def _():
            multiply(i)

        for order, pair in enumerate(((relay, fan), (cross, relay_half), (finish, finish_half))):
            lag = LAG * (order + 1)
            c = i - lag
            inside = (i >= lag) & (c < chunks)

            @pl.when(inside & across_first(c))
            def _():
                pair[1](c)

            @pl.when(inside & jnp.logical_not(across_first(c)))
            def _():
                pair[0](c)

    @pl.loop(0, chunks)
    def _(c):
        @pl.when(across_first(c))
        def _():
            remote_far(c).wait_send()
            for kind in range(6):
                remote_half(kind, c).wait_send()

        @pl.when(jnp.logical_not(across_first(c)))
        def _():
            for kind in range(KINDS):
                remote(kind, c).wait_send()

    for hop in range(len(HOPS)):
        for part in range(parts):
            give(hop, part).wait_send()


def on_device(amplitudes, singles, pair_list, irrep, block_sizes, tile_of_slot, integrals):
    groups = lax.axis_size("ab")
    ring = lax.axis_size("cd") // 2
    local_pairs, columns = amplitudes.shape
    orbitals = irrep.shape[0]
    pairs = local_pairs * groups
    rows = pairs // (2 * ring)
    total = integrals.shape[0]
    width = min(256, orbitals)
    parts = 2
    chunks = total // width
    anywhere = pl.BlockSpec(memory_space=pl.ANY)
    local = pl.BlockSpec(memory_space=pltpu.VMEM)
    scalars = pl.BlockSpec(memory_space=pltpu.SMEM)
    return pl.pallas_call(
        functools.partial(ladder_kernel, ring, width, min(256, width), parts),
        out_shape=jax.ShapeDtypeStruct((rows, total), jnp.float32),
        in_specs=[local, local, local, local, scalars, scalars, scalars, anywhere],
        out_specs=local,
        scratch_shapes=[
            pltpu.VMEM((pairs, columns), jnp.bfloat16),
            pltpu.VMEM((chunks, width, columns), jnp.bfloat16),
            pltpu.VMEM((pairs, width), jnp.float32),
            pltpu.VMEM((4, chunks, rows, width), jnp.float32),
            pltpu.VMEM((KINDS, chunks, rows, width), jnp.bfloat16),
            pltpu.VMEM((KINDS, chunks, rows, width), jnp.bfloat16),
            pltpu.VMEM((chunks // 2, ring, rows, width), jnp.bfloat16),
            pltpu.VMEM((chunks // 2, ring, rows, width), jnp.bfloat16),
            pltpu.VMEM((local_pairs, columns), jnp.bfloat16),
            pltpu.VMEM((local_pairs, orbitals), jnp.float32),
            pltpu.VMEM((local_pairs, 128), jnp.float32),
            pltpu.VMEM((orbitals, 128), jnp.float32),
            pltpu.VMEM((1, columns), jnp.float32),
            pltpu.SemaphoreType.DMA((chunks,)),
            pltpu.SemaphoreType.DMA((KINDS, chunks)),
            pltpu.SemaphoreType.DMA((KINDS, chunks)),
            pltpu.SemaphoreType.DMA((len(HOPS), parts)),
            pltpu.SemaphoreType.DMA((len(HOPS), parts)),
        ],
        compiler_params=pltpu.CompilerParams(
            collective_id=0, has_side_effects=True, vmem_limit_bytes=60 * 1024 * 1024
        ),
    )(
        amplitudes, singles, irrep.reshape(orbitals // 128, 128), pair_list,
        irrep, block_sizes, tile_of_slot, integrals,
    )


def solution(mesh):
    placed = (P("ab", "cd"), P(), P("ab", None), P(), P(), P(), P("ab", "cd"))
    return jax.shard_map(
        on_device, mesh=mesh, in_specs=placed, out_specs=P("cd", "ab"), check_vma=False
    )
```
